32 devices in a mesh: rep: 16 (over z, y, core), grp: 2 (over x).
Axes of the slice: x: 2, y: 2, z: 4, core: 2. Of those that a mesh axis runs over, the one named last changes fastest.
Arguments:
- tokens: bfloat16 [16, 1568, 1024], P('rep', 'grp'), may hold values from -6 to 6
- query_weight: bfloat16 [1024, 1024], P('grp'), may hold values from -0.1875 to 0.1875
- key_weight: bfloat16 [1024, 1024], P('grp'), may hold values from -0.1875 to 0.1875
- value_weight: bfloat16 [1024, 1024], P('grp'), may hold values from -0.1875 to 0.1875
- query_bias: float32 [1024], P('grp'), may hold values from -4 to 4
- value_bias: float32 [1024], P('grp'), may hold values from -0.75 to 0.75
- out_weight: bfloat16 [1024, 1024], P('grp'), may hold values from -4 to 4
- out_bias: float32 [1024], P('grp'), may hold values from -4 to 4
- first_gain: float32 [1024], P('grp'), may hold values from 0.5 to 1.5
- first_shift: float32 [1024], P('grp'), may hold values from -4 to 4
- second_gain: float32 [1024], P('grp'), may hold values from 0.5 to 1.5
- second_shift: float32 [1024], P('grp'), may hold values from -4 to 4
- up_weight: bfloat16 [1024, 4096], P('grp'), may hold values from -0.1875 to 0.1875
- up_bias: float32 [4096], P('grp'), may hold values from -4 to 4
- down_weight: bfloat16 [4096, 1024], P('grp'), may hold values from -0.09375 to 0.09375
- down_bias: float32 [1024], P('grp'), may hold values from -4 to 4
- cotangent: bfloat16 [16, 1568, 1024], P('rep', 'grp'), may hold values from -6 to 6
Outputs:
- layer_out: bfloat16 [16, 1568, 1024], P('rep', 'grp')
- tokens_grad: bfloat16 [16, 1568, 1024], P('rep', 'grp')
- query_weight_grad: float32 [1024, 1024], P('grp')
- key_weight_grad: float32 [1024, 1024], P('grp')
- value_weight_grad: float32 [1024, 1024], P('grp')
- query_bias_grad: float32 [1024], P('grp')
- value_bias_grad: float32 [1024], P('grp')
- out_weight_grad: float32 [1024, 1024], P('grp')
- out_bias_grad: float32 [1024], P('grp')
- first_gain_grad: float32 [1024], P('grp')
- first_shift_grad: float32 [1024], P('grp')
- second_gain_grad: float32 [1024], P('grp')
- second_shift_grad: float32 [1024], P('grp')
- up_weight_grad: float32 [1024, 4096], P('grp')
- up_bias_grad: float32 [4096], P('grp')
- down_weight_grad: float32 [4096, 1024], P('grp')
- down_bias_grad: float32 [1024], P('grp')
The draws below stay inside these ranges and needn't reach their ends.
All inputs are finite; a program needn't handle non-finite values.
Results may differ from the reference program's by a relative error of at most 0.033.
Values may be sent and summed in bfloat16 or wider, within the bound.
No kernel may reach another device: no remote copies, remote signals or barrier semaphores. Data moves between devices by JAX's collectives and lax.ppermute only.
A program may use at most 448 MiB of HBM per device.

```python
import jax
import jax.numpy as jnp
from jax import lax

D = 1024
HEADS = 16
HEAD_DIM = 64
FF = 4096
LEN = 1568
CLIPS = 16


def level_of(key, shape, shards, low, high):
    loudness, own = 1.0, jax.random.fold_in(key, 6)
    for axis_at, blocks in shards:
        steps = jnp.exp(jax.random.uniform(jax.random.fold_in(own, axis_at), (blocks,), jnp.float32, low / len(shards), high / len(shards)))
        loudness = loudness * jnp.repeat(steps, shape[axis_at] // blocks).reshape([-1 if axis == axis_at else 1 for axis in range(len(shape))])
    return loudness


def normal_values(own_key, shape, width, limit, cuts=(), kind=jnp.bfloat16):
    loudness = level_of(own_key, shape, cuts, -0.22, 0.18) if cuts else 1.0
    array = jax.random.normal(own_key, shape, jnp.float32) * width * loudness
    return jnp.minimum(jnp.maximum(array, -limit), limit).astype(kind)


def setup_inputs(seed: int = 0) -> dict:
    splits = jax.random.split(jax.random.key(seed), 18)
    tokens = normal_values(splits[0], (CLIPS, LEN, D), 1.0, 6.0, ((0, 16), (1, 2)))
    query_weight = normal_values(splits[1], (D, D), D ** -0.5, 0.1875, ((0, 2),))
    key_weight = normal_values(splits[2], (D, D), D ** -0.5, 0.1875, ((0, 2),))
    value_weight = normal_values(splits[3], (D, D), D ** -0.5, 0.1875, ((0, 2),))
    query_bias = normal_values(splits[4], (D,), 1.0, 4.0, ((0, 2),), jnp.float32)
    value_bias = normal_values(splits[5], (D,), 0.05, 0.75, ((0, 2),), jnp.float32)
    out_weight = normal_values(splits[6], (D, D), (max(D // 512, 1)) ** -0.5, 4.0, ((0, 2),))
    out_bias = normal_values(splits[7], (D,), 0.5, 4.0, ((0, 2),), jnp.float32)
    first_gain = jnp.clip(1.0 + 0.1 * jax.random.normal(splits[8], (D,), jnp.float32), 0.5, 1.5)
    first_shift = normal_values(splits[9], (D,), 0.3, 4.0, ((0, 2),), jnp.float32)
    second_gain = jnp.clip(1.0 + 0.1 * jax.random.normal(splits[10], (D,), jnp.float32), 0.5, 1.5)
    second_shift = normal_values(splits[11], (D,), 0.3, 4.0, ((0, 2),), jnp.float32)
    up_weight = normal_values(splits[12], (D, FF), D ** -0.5, 0.1875, ((0, 2),))
    up_bias = normal_values(splits[13], (FF,), 0.5, 4.0, ((0, 2),), jnp.float32)
    down_weight = normal_values(splits[14], (FF, D), FF ** -0.5, 0.09375, ((0, 2),))
    down_bias = normal_values(splits[15], (D,), 0.5, 4.0, ((0, 2),), jnp.float32)
    cotangent = normal_values(splits[16], (CLIPS, LEN, D), 1.0, 6.0, ((0, 16), (1, 2)))
    return dict(tokens=tokens, query_weight=query_weight, key_weight=key_weight, value_weight=value_weight, query_bias=query_bias, value_bias=value_bias, out_weight=out_weight, out_bias=out_bias, first_gain=first_gain, first_shift=first_shift, second_gain=second_gain, second_shift=second_shift, up_weight=up_weight, up_bias=up_bias, down_weight=down_weight, down_bias=down_bias, cotangent=cotangent)


@jax.custom_vjp
def low(v):
    return lax.optimization_barrier(v.astype(jnp.bfloat16)).astype(jnp.float32)

@jax.custom_vjp
def low_back(v):
    return v

def low_keep(v):
    return (low(v), None)

def low_pass(kept, grad):
    return (grad,)

def back_keep(v):
    return (v, None)

def back_low(kept, grad):
    return (low(grad),)
low.defvjp(low_keep, low_pass)
low_back.defvjp(back_keep, back_low)
EPS = 1e-06
HIGH = lax.Precision.HIGHEST

def norm_rows(values, gain, shift):
    average = lax.optimization_barrier(jnp.mean(values, axis=-1, keepdims=True))
    centred = values - average
    spread = lax.optimization_barrier(jnp.mean(centred * centred, axis=-1, keepdims=True))
    return centred * lax.rsqrt(spread + EPS) * gain + shift

def product(left, right):
    return jnp.dot(left, right, precision=HIGH)

def clip_layer(params, clip):
    query_weight, key_weight, value_weight, query_bias, value_bias, out_weight, out_bias, first_gain, first_shift, second_gain, second_shift, up_weight, up_bias, down_weight, down_bias = params
    length = clip.shape[0]
    first = low(norm_rows(clip, first_gain, first_shift))
    query = low(low_back(product(first, query_weight) + query_bias)).reshape(length, HEADS, HEAD_DIM)
    key = low(low_back(product(first, key_weight))).reshape(length, HEADS, HEAD_DIM)
    value = low(low_back(product(first, value_weight) + value_bias)).reshape(length, HEADS, HEAD_DIM)
    scale = HEAD_DIM ** (-0.5)
    scores = low_back(jnp.einsum('qhd,khd->hqk', query, key, precision=HIGH) * scale)
    probs = low(jax.nn.softmax(scores, axis=-1))
    mixed = jnp.einsum('hqk,khd->qhd', probs, value, precision=HIGH).reshape(length, D)
    mixed = low(low_back(mixed))
    middle = clip + low_back(product(mixed, out_weight) + out_bias)
    second = low(norm_rows(middle, second_gain, second_shift))
    pre = low_back(product(second, up_weight) + up_bias)
    hidden = low(jax.nn.gelu(pre, approximate=False))
    return middle + product(hidden, down_weight) + down_bias

def reference(tokens, query_weight, key_weight, value_weight, query_bias, value_bias, out_weight, out_bias, first_gain, first_shift, second_gain, second_shift, up_weight, up_bias, down_weight, down_bias, cotangent):
    params = tuple((item.astype(jnp.float32) for item in (query_weight, key_weight, value_weight, query_bias, value_bias, out_weight, out_bias, first_gain, first_shift, second_gain, second_shift, up_weight, up_bias, down_weight, down_bias)))
    inputs = tokens.astype(jnp.float32)

    def forward(weights, clips):

        def one_clip(clip):
            return clip_layer(weights, clip)
        return lax.map(jax.checkpoint(one_clip), clips)
    result, pullback = jax.vjp(forward, params, inputs)
    grads, input_grad = pullback(cotangent.astype(jnp.float32))
    return (result.astype(jnp.bfloat16), input_grad.astype(jnp.bfloat16), grads[0], grads[1], grads[2], grads[3], grads[4], grads[5], grads[6], grads[7], grads[8], grads[9], grads[10], grads[11], grads[12], grads[13], grads[14])
```

```python
from functools import partial

import jax
import jax.numpy as jnp
from jax import lax
from jax.sharding import PartitionSpec as P

HEAD_DIM = 64


EPS = 1e-06


def norm_parts(values, gain, shift):
    average = jnp.mean(values, axis=-1, keepdims=True)
    centred = values - average
    spread = jnp.mean(centred * centred, axis=-1, keepdims=True)
    inverse = lax.rsqrt(spread + EPS)
    normed = centred * inverse
    return (normed * gain + shift, normed, inverse)


def norm_back(grad, normed, inverse, gain):
    scaled = grad * gain
    first_term = jnp.mean(scaled, axis=-1, keepdims=True)
    second_term = jnp.mean(scaled * normed, axis=-1, keepdims=True)
    result = inverse * (scaled - first_term - normed * second_term)
    return (result, jnp.sum(grad * normed, axis=0), jnp.sum(grad, axis=0))


def matmul(left, right):
    return jnp.dot(left, right, preferred_element_type=jnp.float32)


def matmul_right_t(left, right):
    return lax.dot_general(
        left, right, (((1,), (1,)), ((), ())), preferred_element_type=jnp.float32
    )


def matmul_left_t(left, right):
    return lax.dot_general(
        left, right, (((0,), (0,)), ((), ())), preferred_element_type=jnp.float32
    )


def split_heads(values):
    return values.reshape(values.shape[0], values.shape[1] // HEAD_DIM, HEAD_DIM)


def attend_clip(operands):
    queries, keys, values = operands
    scale = HEAD_DIM ** (-0.5)
    scores = (
        jnp.einsum(
            "qhd,khd->hqk",
            split_heads(queries),
            split_heads(keys),
            preferred_element_type=jnp.float32,
        )
        * scale
    )
    highest = jnp.max(scores, axis=-1, keepdims=True)
    expon = jnp.exp(scores - highest)
    totals = jnp.sum(expon, axis=-1, keepdims=True)
    probs = (expon / totals).astype(jnp.bfloat16)
    mixed = jnp.einsum(
        "hqk,khd->qhd", probs, split_heads(values), preferred_element_type=jnp.float32
    )
    return (
        mixed.reshape(queries.shape[0], queries.shape[1]),
        highest[..., 0] + jnp.log(totals[..., 0]),
    )


def attend_back(operands):
    queries, keys, values, grad_mixed, log_total = operands
    scale = HEAD_DIM ** (-0.5)
    query_heads = split_heads(queries)
    key_heads = split_heads(keys)
    grad_heads = split_heads(grad_mixed)
    scores = (
        jnp.einsum("qhd,khd->hqk", query_heads, key_heads, preferred_element_type=jnp.float32)
        * scale
    )
    weights = jnp.exp(scores - log_total[..., None])
    probs = weights.astype(jnp.bfloat16)
    grad_probs = jnp.einsum(
        "qhd,khd->hqk", grad_heads, split_heads(values), preferred_element_type=jnp.float32
    )
    grad_values = jnp.einsum("hqk,qhd->khd", probs, grad_heads, preferred_element_type=jnp.float32)
    inner = jnp.sum(grad_probs * weights, axis=-1, keepdims=True)
    grad_scores = (weights * (grad_probs - inner)).astype(jnp.bfloat16)
    grad_queries = (
        jnp.einsum("hqk,khd->qhd", grad_scores, key_heads, preferred_element_type=jnp.float32)
        * scale
    )
    grad_keys = (
        jnp.einsum("hqk,qhd->khd", grad_scores, query_heads, preferred_element_type=jnp.float32)
        * scale
    )
    return (
        grad_queries.reshape(queries.shape[0], queries.shape[1]),
        grad_keys.reshape(keys.shape[0], keys.shape[1]),
        grad_values.reshape(keys.shape[0], keys.shape[1]),
    )


def spread_body(
    tokens,
    query_weight,
    key_weight,
    value_weight,
    query_bias,
    value_bias,
    out_weight,
    out_bias,
    first_gain,
    first_shift,
    second_gain,
    second_shift,
    up_weight,
    up_bias,
    down_weight,
    down_bias,
    cotangent,
):
    clips, local_len, width = tokens.shape
    rows = clips * local_len
    attention_set = (
        lax.all_gather(query_weight, "grp", axis=0, tiled=True),
        lax.all_gather(key_weight, "grp", axis=0, tiled=True),
        lax.all_gather(value_weight, "grp", axis=0, tiled=True),
        lax.all_gather(query_bias.astype(jnp.bfloat16), "grp", axis=0, tiled=True).astype(
            query_bias.dtype
        ),
        lax.all_gather(value_bias.astype(jnp.bfloat16), "grp", axis=0, tiled=True).astype(
            value_bias.dtype
        ),
        lax.all_gather(out_weight, "grp", axis=0, tiled=True),
        lax.all_gather(out_bias.astype(jnp.bfloat16), "grp", axis=0, tiled=True).astype(
            out_bias.dtype
        ),
        lax.all_gather(first_gain.astype(jnp.bfloat16), "grp", axis=0, tiled=True).astype(
            first_gain.dtype
        ),
        lax.all_gather(first_shift.astype(jnp.bfloat16), "grp", axis=0, tiled=True).astype(
            first_shift.dtype
        ),
    )
    feed_set = (
        lax.all_gather(second_gain.astype(jnp.bfloat16), "grp", axis=0, tiled=True).astype(
            second_gain.dtype
        ),
        lax.all_gather(second_shift.astype(jnp.bfloat16), "grp", axis=0, tiled=True).astype(
            second_shift.dtype
        ),
        lax.all_gather(up_weight, "grp", axis=0, tiled=True),
        lax.all_gather(up_bias.astype(jnp.bfloat16), "grp", axis=0, tiled=True).astype(
            up_bias.dtype
        ),
        lax.all_gather(down_weight, "grp", axis=0, tiled=True),
        lax.all_gather(down_bias.astype(jnp.bfloat16), "grp", axis=0, tiled=True).astype(
            down_bias.dtype
        ),
    )
    (
        full_query,
        full_key,
        full_value,
        full_qbias,
        full_vbias,
        full_out,
        full_obias,
        full_gain_one,
        full_shift_one,
    ) = attention_set
    full_gain_two, full_shift_two, full_up, full_ubias, full_down, full_dbias = feed_set
    inputs = tokens.reshape(rows, width).astype(jnp.float32)
    first_norm, first_normed, first_inverse = norm_parts(inputs, full_gain_one, full_shift_one)
    first_low = first_norm.astype(jnp.bfloat16)
    query_low = (matmul(first_low, full_query) + full_qbias).astype(jnp.bfloat16)
    key_low = matmul(first_low, full_key).astype(jnp.bfloat16)
    value_low = (matmul(first_low, full_value) + full_vbias).astype(jnp.bfloat16)
    query_clips = query_low.reshape(clips, local_len, width)
    key_clips = key_low.reshape(clips, local_len, width)
    value_clips = value_low.reshape(clips, local_len, width)
    key_whole, value_whole = (
        lax.all_gather(key_clips, "grp", axis=1, tiled=True),
        lax.all_gather(value_clips, "grp", axis=1, tiled=True),
    )
    mixed, log_total = lax.map(attend_clip, (query_clips, key_whole, value_whole))
    mixed_low = mixed.reshape(rows, width).astype(jnp.bfloat16)
    middle = inputs + matmul(mixed_low, full_out) + full_obias
    second_norm, second_normed, second_inverse = norm_parts(middle, full_gain_two, full_shift_two)
    second_low = second_norm.astype(jnp.bfloat16)
    hidden_pre = matmul(second_low, full_up) + full_ubias
    hidden_low = jax.nn.gelu(hidden_pre, approximate=False).astype(jnp.bfloat16)
    result = middle + matmul(hidden_low, full_down) + full_dbias
    layer_out = result.astype(jnp.bfloat16).reshape(clips, local_len, width)
    attention_back = (
        lax.all_gather(query_weight, "grp", axis=0, tiled=True),
        lax.all_gather(key_weight, "grp", axis=0, tiled=True),
        lax.all_gather(value_weight, "grp", axis=0, tiled=True),
        lax.all_gather(query_bias.astype(jnp.bfloat16), "grp", axis=0, tiled=True).astype(
            query_bias.dtype
        ),
        lax.all_gather(value_bias.astype(jnp.bfloat16), "grp", axis=0, tiled=True).astype(
            value_bias.dtype
        ),
        lax.all_gather(out_weight, "grp", axis=0, tiled=True),
        lax.all_gather(out_bias.astype(jnp.bfloat16), "grp", axis=0, tiled=True).astype(
            out_bias.dtype
        ),
        lax.all_gather(first_gain.astype(jnp.bfloat16), "grp", axis=0, tiled=True).astype(
            first_gain.dtype
        ),
        lax.all_gather(first_shift.astype(jnp.bfloat16), "grp", axis=0, tiled=True).astype(
            first_shift.dtype
        ),
    )
    feed_back = (
        lax.all_gather(second_gain.astype(jnp.bfloat16), "grp", axis=0, tiled=True).astype(
            second_gain.dtype
        ),
        lax.all_gather(second_shift.astype(jnp.bfloat16), "grp", axis=0, tiled=True).astype(
            second_shift.dtype
        ),
        lax.all_gather(up_weight, "grp", axis=0, tiled=True),
        lax.all_gather(up_bias.astype(jnp.bfloat16), "grp", axis=0, tiled=True).astype(
            up_bias.dtype
        ),
        lax.all_gather(down_weight, "grp", axis=0, tiled=True),
        lax.all_gather(down_bias.astype(jnp.bfloat16), "grp", axis=0, tiled=True).astype(
            down_bias.dtype
        ),
    )
    (
        back_query,
        back_key,
        back_value,
        unused_qbias,
        unused_vbias,
        back_out,
        unused_obias,
        back_gain_one,
        unused_shift_one,
    ) = attention_back
    back_gain_two, unused_shift_two, back_up, unused_ubias, back_down, unused_dbias = feed_back
    grad_out = cotangent.reshape(rows, width)
    grad_out_wide = grad_out.astype(jnp.float32)
    grad_hidden = matmul_right_t(grad_out, back_down)
    grad_down_weight = matmul_left_t(hidden_low, grad_out)
    grad_down_bias = jnp.sum(grad_out_wide, axis=0)
    unused_value, gelu_pull = jax.vjp(partial(jax.nn.gelu, approximate=False), hidden_pre)
    grad_pre_low = gelu_pull(grad_hidden)[0].astype(jnp.bfloat16)
    grad_up_weight = matmul_left_t(second_low, grad_pre_low)
    grad_up_bias = jnp.sum(grad_pre_low.astype(jnp.float32), axis=0)
    grad_second, grad_gain_two, grad_shift_two = norm_back(
        matmul_right_t(grad_pre_low, back_up), second_normed, second_inverse, back_gain_two
    )
    grad_middle = grad_out_wide + grad_second
    grad_middle_low = grad_middle.astype(jnp.bfloat16)
    grad_out_weight = matmul_left_t(mixed_low, grad_middle_low)
    grad_out_bias = jnp.sum(grad_middle_low.astype(jnp.float32), axis=0)
    grad_mixed_low = matmul_right_t(grad_middle_low, back_out).astype(jnp.bfloat16)
    grad_mixed_clips = grad_mixed_low.reshape(clips, local_len, width)
    grad_queries, grad_keys, grad_values = lax.map(
        attend_back, (query_clips, key_whole, value_whole, grad_mixed_clips, log_total)
    )
    key_share, value_share = (
        lax.psum_scatter(
            grad_keys.astype(jnp.bfloat16), "grp", scatter_dimension=1, tiled=True
        ).astype(jnp.float32),
        lax.psum_scatter(
            grad_values.astype(jnp.bfloat16), "grp", scatter_dimension=1, tiled=True
        ).astype(jnp.float32),
    )
    query_grad_low = grad_queries.reshape(rows, width).astype(jnp.bfloat16)
    key_grad_low = key_share.reshape(rows, width).astype(jnp.bfloat16)
    value_grad_low = value_share.reshape(rows, width).astype(jnp.bfloat16)
    grad_query_weight = matmul_left_t(first_low, query_grad_low)
    grad_key_weight = matmul_left_t(first_low, key_grad_low)
    grad_value_weight = matmul_left_t(first_low, value_grad_low)
    grad_query_bias = jnp.sum(query_grad_low.astype(jnp.float32), axis=0)
    grad_value_bias = jnp.sum(value_grad_low.astype(jnp.float32), axis=0)
    grad_first_norm = (
        matmul_right_t(query_grad_low, back_query)
        + matmul_right_t(key_grad_low, back_key)
        + matmul_right_t(value_grad_low, back_value)
    )
    grad_first, grad_gain_one, grad_shift_one = norm_back(
        grad_first_norm, first_normed, first_inverse, back_gain_one
    )
    tokens_grad = (grad_middle + grad_first).astype(jnp.bfloat16).reshape(clips, local_len, width)
    shares = (
        lax.psum_scatter(
            grad_query_weight.astype(jnp.bfloat16), "grp", scatter_dimension=0, tiled=True
        ).astype(jnp.float32),
        lax.psum_scatter(
            grad_key_weight.astype(jnp.bfloat16), "grp", scatter_dimension=0, tiled=True
        ).astype(jnp.float32),
        lax.psum_scatter(
            grad_value_weight.astype(jnp.bfloat16), "grp", scatter_dimension=0, tiled=True
        ).astype(jnp.float32),
        lax.psum_scatter(
            grad_query_bias.astype(jnp.bfloat16), "grp", scatter_dimension=0, tiled=True
        ).astype(jnp.float32),
        lax.psum_scatter(
            grad_value_bias.astype(jnp.bfloat16), "grp", scatter_dimension=0, tiled=True
        ).astype(jnp.float32),
        lax.psum_scatter(
            grad_out_weight.astype(jnp.bfloat16), "grp", scatter_dimension=0, tiled=True
        ).astype(jnp.float32),
        lax.psum_scatter(
            grad_out_bias.astype(jnp.bfloat16), "grp", scatter_dimension=0, tiled=True
        ).astype(jnp.float32),
        lax.psum_scatter(
            grad_gain_one.astype(jnp.bfloat16), "grp", scatter_dimension=0, tiled=True
        ).astype(jnp.float32),
        lax.psum_scatter(
            grad_shift_one.astype(jnp.bfloat16), "grp", scatter_dimension=0, tiled=True
        ).astype(jnp.float32),
        lax.psum_scatter(
            grad_gain_two.astype(jnp.bfloat16), "grp", scatter_dimension=0, tiled=True
        ).astype(jnp.float32),
        lax.psum_scatter(
            grad_shift_two.astype(jnp.bfloat16), "grp", scatter_dimension=0, tiled=True
        ).astype(jnp.float32),
        lax.psum_scatter(
            grad_up_weight.astype(jnp.bfloat16), "grp", scatter_dimension=0, tiled=True
        ).astype(jnp.float32),
        lax.psum_scatter(
            grad_up_bias.astype(jnp.bfloat16), "grp", scatter_dimension=0, tiled=True
        ).astype(jnp.float32),
        lax.psum_scatter(
            grad_down_weight.astype(jnp.bfloat16), "grp", scatter_dimension=0, tiled=True
        ).astype(jnp.float32),
        lax.psum_scatter(
            grad_down_bias.astype(jnp.bfloat16), "grp", scatter_dimension=0, tiled=True
        ).astype(jnp.float32),
    )
    totals = (
        lax.psum(shares[0].astype(jnp.bfloat16), "rep").astype(jnp.float32),
        lax.psum(shares[1].astype(jnp.bfloat16), "rep").astype(jnp.float32),
        lax.psum(shares[2].astype(jnp.bfloat16), "rep").astype(jnp.float32),
        lax.psum(shares[3].astype(jnp.bfloat16), "rep").astype(jnp.float32),
        lax.psum(shares[4].astype(jnp.bfloat16), "rep").astype(jnp.float32),
        lax.psum(shares[5].astype(jnp.bfloat16), "rep").astype(jnp.float32),
        lax.psum(shares[6].astype(jnp.bfloat16), "rep").astype(jnp.float32),
        lax.psum(shares[7].astype(jnp.bfloat16), "rep").astype(jnp.float32),
        lax.psum(shares[8].astype(jnp.bfloat16), "rep").astype(jnp.float32),
        lax.psum(shares[9].astype(jnp.bfloat16), "rep").astype(jnp.float32),
        lax.psum(shares[10].astype(jnp.bfloat16), "rep").astype(jnp.float32),
        lax.psum(shares[11].astype(jnp.bfloat16), "rep").astype(jnp.float32),
        lax.psum(shares[12].astype(jnp.bfloat16), "rep").astype(jnp.float32),
        lax.psum(shares[13].astype(jnp.bfloat16), "rep").astype(jnp.float32),
        lax.psum(shares[14].astype(jnp.bfloat16), "rep").astype(jnp.float32),
    )
    return (
        layer_out,
        tokens_grad,
        totals[0],
        totals[1],
        totals[2],
        totals[3],
        totals[4],
        totals[5],
        totals[6],
        totals[7],
        totals[8],
        totals[9],
        totals[10],
        totals[11],
        totals[12],
        totals[13],
        totals[14],
    )


def flip(values, axis, size, bit):
    mask = 1 << bit
    return lax.ppermute(values, axis, [(at, at ^ mask) for at in range(size)])


def ordered(mine, theirs, place, axis=0):
    first = jnp.where(place == 0, mine, theirs)
    last = jnp.where(place == 0, theirs, mine)
    return jnp.concatenate((first, last), axis=axis)


def pick_part(values, place):
    rows, width = values.shape
    blocks = values.reshape(rows, 2, 2, width // 4)
    return lax.dynamic_index_in_dim(blocks, place, axis=2, keepdims=False).reshape(
        rows, width // 2
    )


def join_parts(mine, theirs, place):
    rows, width = mine.shape
    mine = mine.reshape(rows, 2, 1, width // 2)
    theirs = theirs.reshape(rows, 2, 1, width // 2)
    return ordered(mine, theirs, place, axis=2).reshape(rows, 2 * width)


def paired_body(
    rep_size,
    tokens,
    query_weight,
    key_weight,
    value_weight,
    query_bias,
    value_bias,
    out_weight,
    out_bias,
    first_gain,
    first_shift,
    second_gain,
    second_shift,
    up_weight,
    up_bias,
    down_weight,
    down_bias,
    cotangent,
):
    low = jnp.bfloat16
    wide = jnp.float32
    rep_bits = rep_size.bit_length() - 1
    rep_at = lax.axis_index("rep")
    grp_at = lax.axis_index("grp")
    core_at = rep_at & 1
    length, width = tokens.shape[1], tokens.shape[2]
    shard = width // 2
    devices = [(rep, grp) for rep in range(rep_size) for grp in range(2)]
    swap = [
        (2 * rep + grp, 2 * (rep - rep % 2 + grp) + rep % 2)
        for rep, grp in devices
        if rep % 2 != grp
    ]

    def swap_clips(values):
        moved = lax.ppermute(values, ("rep", "grp"), swap)
        return jnp.where(core_at == grp_at, values, moved)

    def over_core(values):
        return flip(values, "rep", rep_size, 0)

    def over_group(values):
        return flip(values, "grp", 2, 0)

    vectors = (
        query_bias,
        value_bias,
        out_bias,
        first_gain,
        first_shift,
        second_gain,
        second_shift,
        up_bias,
        down_bias,
    )
    packed = jnp.concatenate(vectors).reshape(-1, 128)
    packed_two = ordered(packed[None], over_group(packed)[None], grp_at).reshape(2, -1)
    whole, start = [], 0
    for vector in vectors:
        whole.append(packed_two[:, start : start + vector.shape[0]].reshape(-1))
        start += vector.shape[0]
    qbias, vbias, obias, gain_one, shift_one, gain_two, shift_two, ubias, dbias = whole

    own_qkv = jnp.concatenate(
        [pick_part(item, core_at) for item in (query_weight, key_weight, value_weight)], axis=1
    )
    if rep_bits > 1:
        half = shard // 2
        row_at = (rep_at >> 1) & 1
        piece = over_group(lax.dynamic_slice_in_dim(own_qkv, row_at * half, half, 0))
        other_qkv = ordered(piece, flip(piece, "rep", rep_size, 1), row_at)
    else:
        other_qkv = over_group(own_qkv)
    tokens_own = swap_clips(tokens[0])
    full_qkv = ordered(own_qkv, other_qkv, grp_at)
    bias_qkv = jnp.concatenate(
        (
            pick_part(qbias[None], core_at)[0],
            jnp.zeros((shard,), wide),
            pick_part(vbias[None], core_at)[0],
        )
    )
    grad_own = swap_clips(cotangent[0])

    def gather_weight(weight, after):
        rows = weight.shape[0] // rep_size
        piece = lax.dynamic_slice_in_dim(weight, rep_at * rows, rows, 0)
        piece, _ = lax.optimization_barrier((piece, after))
        return lax.all_gather(piece, ("grp", "rep"), axis=0, tiled=True)

    full_out = gather_weight(out_weight, tokens_own)
    full_up = gather_weight(up_weight, tokens_own)
    full_down = gather_weight(down_weight, tokens_own)

    inputs = tokens_own.astype(wide)
    first_norm, first_normed, first_inverse = norm_parts(inputs, gain_one, shift_one)
    first_low = first_norm.astype(low)
    first_all = jnp.concatenate((first_low, over_core(first_low)), axis=0)
    qkv = (matmul(first_all, full_qkv) + bias_qkv).astype(low)
    queries, keys, values = qkv[:, :shard], qkv[:, shard : 2 * shard], qkv[:, 2 * shard :]
    mixed_heads, log_total = attend_clip((queries, keys, values))
    mixed_heads = mixed_heads.astype(low)
    mixed_low = join_parts(mixed_heads[:length], over_core(mixed_heads[length:]), core_at)
    middle = inputs + matmul(mixed_low, full_out) + obias
    second_norm, second_normed, second_inverse = norm_parts(middle, gain_two, shift_two)
    second_low = second_norm.astype(low)
    hidden_pre = matmul(second_low, full_up) + ubias
    hidden_low = jax.nn.gelu(hidden_pre, approximate=False).astype(low)
    result = middle + matmul(hidden_low, full_down) + dbias
    layer_out = swap_clips(result.astype(low))[None]

    def both(values):
        return jnp.concatenate((values, over_core(values)), axis=0)

    def both_parts(values):
        mine = pick_part(values, core_at)
        return jnp.concatenate((mine, over_core(pick_part(values, 1 - core_at))), axis=0)

    def column_half(values, place):
        half = values.shape[1] // 2
        return lax.dynamic_slice_in_dim(values, place * half, half, 1)

    def add_up(left, right):
        give = matmul_left_t(column_half(left, 1 - grp_at), right).astype(low)
        part = matmul_left_t(column_half(left, grp_at), right) + over_group(give).astype(wide)
        for bit in range(1, rep_bits):
            half = part.shape[0] // 2
            at = (rep_at >> bit) & 1
            give = lax.dynamic_slice_in_dim(part, (1 - at) * half, half, 0).astype(low)
            keep = lax.dynamic_slice_in_dim(part, at * half, half, 0)
            part = keep + flip(give, "rep", rep_size, bit).astype(wide)
        total = part.astype(low)
        for bit in reversed(range(1, rep_bits)):
            total = ordered(total, flip(total, "rep", rep_size, bit), (rep_at >> bit) & 1)
        return total, over_core(total)

    grad_wide = grad_own.astype(wide)
    grad_all = both(grad_own)
    down_total = add_up(both_parts(hidden_low), grad_all)
    grad_hidden = matmul_right_t(grad_own, full_down)
    unused_value, gelu_pull = jax.vjp(partial(jax.nn.gelu, approximate=False), hidden_pre)
    grad_pre_low = gelu_pull(grad_hidden)[0].astype(low)
    up_total = add_up(both(second_low), both_parts(grad_pre_low))
    grad_second, grad_gain_two, grad_shift_two = norm_back(
        matmul_right_t(grad_pre_low, full_up), second_normed, second_inverse, gain_two
    )
    grad_middle = grad_wide + grad_second
    grad_middle_low = grad_middle.astype(low)
    out_total = add_up(mixed_heads, both(grad_middle_low))
    early = (
        jnp.sum(grad_middle_low.astype(wide), axis=0),
        grad_gain_two,
        grad_shift_two,
        jnp.sum(grad_pre_low.astype(wide), axis=0),
        jnp.sum(grad_wide, axis=0),
    )
    grad_mixed_low = matmul_right_t(grad_middle_low, full_out).astype(low)
    grad_mixed_heads = both_parts(grad_mixed_low)
    grad_queries, grad_keys, grad_values = attend_back(
        (queries, keys, values, grad_mixed_heads, log_total)
    )
    grad_qkv = jnp.concatenate((grad_queries, grad_keys, grad_values), axis=1).astype(low)
    qkv_total = add_up(first_all, grad_qkv)
    partial_first = matmul_right_t(grad_qkv[length:], full_qkv).astype(low)
    grad_first_norm = matmul_right_t(grad_qkv[:length], full_qkv) + over_core(
        partial_first
    ).astype(wide)
    grad_first, grad_gain_one, grad_shift_one = norm_back(
        grad_first_norm, first_normed, first_inverse, gain_one
    )
    tokens_grad = swap_clips((grad_middle + grad_first).astype(low))[None]

    head_bias = jnp.sum(grad_qkv.astype(wide), axis=0)
    nothing = jnp.zeros((1, shard), wide)
    late = (
        join_parts(head_bias[None, :shard], nothing, core_at)[0],
        join_parts(head_bias[None, 2 * shard :], nothing, core_at)[0],
        grad_gain_one,
        grad_shift_one,
    )

    def sum_vectors(items):
        total = lax.psum(jnp.concatenate(items), ("rep", "grp"))
        out, start = [], 0
        for item in items:
            size = item.shape[0] // 2
            out.append(lax.dynamic_slice_in_dim(total, start + grp_at * size, size, 0))
            start += 2 * size
        return out

    obias_grad, gain_two_grad, shift_two_grad, ubias_grad, dbias_grad = sum_vectors(early)
    qbias_grad, vbias_grad, gain_one_grad, shift_one_grad = sum_vectors(late)

    def wide_rows(pair):
        return ordered(pair[0], pair[1], core_at).astype(wide)

    def wide_columns(mine, theirs):
        return join_parts(mine, theirs, core_at).astype(wide)

    qkv_mine, qkv_theirs = qkv_total
    return (
        layer_out,
        tokens_grad,
        wide_columns(qkv_mine[:, :shard], qkv_theirs[:, :shard]),
        wide_columns(qkv_mine[:, shard : 2 * shard], qkv_theirs[:, shard : 2 * shard]),
        wide_columns(qkv_mine[:, 2 * shard :], qkv_theirs[:, 2 * shard :]),
        qbias_grad,
        vbias_grad,
        wide_rows(out_total),
        obias_grad,
        gain_one_grad,
        shift_one_grad,
        gain_two_grad,
        shift_two_grad,
        wide_columns(*up_total),
        ubias_grad,
        wide_rows(down_total),
        dbias_grad,
    )


def solution(mesh):
    rep_size = mesh.shape["rep"]
    paired = mesh.shape["grp"] == 2 and rep_size > 1 and rep_size & (rep_size - 1) == 0
    body = partial(paired_body, rep_size) if paired else spread_body
    placed = (
        P("rep", "grp", None),
        P("grp", None),
        P("grp", None),
        P("grp", None),
        P("grp"),
        P("grp"),
        P("grp", None),
        P("grp"),
        P("grp"),
        P("grp"),
        P("grp"),
        P("grp"),
        P("grp", None),
        P("grp"),
        P("grp", None),
        P("grp"),
        P("rep", "grp", None),
    )
    return jax.shard_map(
        body,
        mesh=mesh,
        in_specs=placed,
        out_specs=(
            P("rep", "grp", None),
            P("rep", "grp", None),
            P("grp", None),
            P("grp", None),
            P("grp", None),
            P("grp"),
            P("grp"),
            P("grp", None),
            P("grp"),
            P("grp"),
            P("grp"),
            P("grp"),
            P("grp"),
            P("grp", None),
            P("grp"),
            P("grp", None),
            P("grp"),
        ),
        check_vma=False,
    )
```
